32 devices in a mesh: chi: 4 (over y, x), dl: 4 (over z), cell: 2 (over core).
Axes of the slice: x: 2, y: 2, z: 4, core: 2. Of those that a mesh axis runs over, the one named last changes fastest.
Arguments:
- left_env: bfloat16 [2, 512, 512, 36], P('cell', None, 'chi'), may hold values from -6 to 6
- up_left: bfloat16 [2, 512, 36, 512], P('cell', 'chi', None, 'dl'), may hold values from -0.109375 to 0.109375
- up_center: bfloat16 [2, 512, 36, 512], P('cell', 'chi', None, 'dl'), may hold values from -0.109375 to 0.109375
- right_env: bfloat16 [2, 512, 36, 512], P('cell', 'dl'), may hold values from -0.046875 to 0.046875
- center: bfloat16 [2, 512, 512], P('cell', None, 'dl'), may hold values from -0.25 to 0.25
- ket_tensor: bfloat16 [2, 6, 6, 6, 6, 2], P('cell'), may hold values from -0.875 to 0.875
Outputs:
- left_env_new: float32 [2, 512, 36, 512], P('cell', 'chi', None, 'dl')
- new_left: float32 [2, 512, 36, 512], P('cell', 'chi', None, 'dl')
The draws below stay inside these ranges and needn't reach their ends.
All inputs are finite; a program needn't handle non-finite values.
Results may differ from the reference program's by a relative error of at most 0.0066.
The reference program's roundings to bfloat16 on the way count: a program that leaves them out, or rounds other values in their place, can miss the bound.
Values may be sent and summed in bfloat16 or wider, within the bound.
A program may use at most 256 MiB of HBM per device.

```python
import math
import jax
import jax.numpy as jnp
from jax import lax

CHI = 512
D = 6
PHYS = 2
ITERS = 5
DL = 36
ROWS = 2


def block_scale(rng, shape, cuts, low, high):
    def one(position, blocks):
        draws = jax.random.uniform(jax.random.fold_in(jax.random.fold_in(rng, 6), position), (blocks,), jnp.float32, low / len(cuts), high / len(cuts))
        return jnp.repeat(jnp.exp(draws), shape[position] // blocks).reshape((-1,) + (1,) * (len(shape) - position - 1))

    factor_of = one(*cuts[0])
    for cut in cuts[1:]:
        factor_of = factor_of * one(*cut)
    return factor_of


def normal_values(stream_key, dims, deviation, reach, split=(), kind=jnp.bfloat16):
    entries = jax.random.normal(stream_key, dims, jnp.float32) * deviation
    if len(split) > 0:
        entries = block_scale(stream_key, dims, split, -0.22, 0.18) * entries
    return jnp.clip(entries, min=-reach, max=reach).astype(kind)


def setup_inputs(seed: int = 0) -> dict:
    key_list = jax.random.split(jax.random.key(seed), 7)
    left_env = normal_values(key_list[0], (ROWS, CHI, CHI, DL), 1.0, 6.0, ((0, 2), (2, 4)))
    up_left = normal_values(key_list[1], (ROWS, CHI, DL, CHI), (CHI * D) ** -0.5, 0.109375, ((0, 2), (1, 4), (3, 4)))
    up_center = normal_values(key_list[2], (ROWS, CHI, DL, CHI), (CHI * D) ** -0.5, 0.109375, ((0, 2), (1, 4), (3, 4)))
    right_env = normal_values(key_list[3], (ROWS, CHI, DL, CHI), (CHI * DL) ** -0.5, 0.046875, ((0, 2), (1, 4)))
    center = normal_values(key_list[4], (ROWS, CHI, CHI), CHI ** -0.5, 0.25, ((0, 2), (2, 4)))
    ket_tensor = normal_values(key_list[5], (ROWS, D, D, D, D, PHYS), 50 ** -0.5, 0.875, ((0, 2),))
    return {"left_env": left_env, "up_left": up_left, "up_center": up_center, "right_env": right_env, "center": center, "ket_tensor": ket_tensor}


HIGHEST = lax.Precision.HIGHEST

def layered(block, tensor):
    leg_size = tensor.shape[0]
    amount = block.shape[0]
    columns = block.shape[3]
    unfolded = block.reshape(amount, leg_size, leg_size, leg_size, leg_size, columns).astype(jnp.float32)
    tensor_f = tensor.astype(jnp.float32)
    ket_side = jnp.einsum('blLuUc,lurdp->bLUcrdp', unfolded, tensor_f).astype(jnp.bfloat16)
    both_sides = jnp.einsum('bLUcrdp,LUsep->brsdec', ket_side.astype(jnp.float32), tensor_f)
    return both_sides.reshape(amount, leg_size * leg_size, leg_size * leg_size, columns).astype(jnp.bfloat16)

def one_row(env_left, left_iso, left_mid, env_right, bond_mat, site_ket, bra_iso):
    chi_all = env_left.shape[0]
    leg_width = env_left.shape[2]
    stride = min(chi_all, 32)
    blocks = chi_all // stride
    env_blocks = jnp.moveaxis(env_left.reshape(chi_all, blocks, stride, leg_width), 1, 0)
    bra_blocks = bra_iso.reshape(blocks, stride, leg_width, chi_all)
    iso_f = left_iso.astype(jnp.float32)
    mid_f = left_mid.astype(jnp.float32)
    right_f = env_right.astype(jnp.float32)

    def visit(running, pieces):
        env_block, bra_block = pieces
        env_f = env_block.astype(jnp.float32)
        left_x = jnp.einsum('abm,asc->bmsc', env_f, iso_f).astype(jnp.bfloat16)
        right_x = jnp.einsum('abm,asc->bmsc', env_f, mid_f).astype(jnp.bfloat16)
        left_cut = layered(left_x, site_ket)
        right_cut = layered(right_x, site_ket)
        running = running + jnp.einsum('bmdc,bdk->kmc', left_cut.astype(jnp.float32), bra_block.astype(jnp.float32))
        center_piece = jnp.einsum('bmda,amc->cbd', right_cut.astype(jnp.float32), right_f)
        return (running, center_piece)
    initial = jnp.zeros((chi_all, leg_width, chi_all), jnp.float32)
    env_new, center_pieces = lax.scan(visit, initial, (env_blocks, bra_blocks))
    center_new = jnp.moveaxis(center_pieces, 0, 1).reshape(chi_all, chi_all, leg_width).astype(jnp.bfloat16)
    mixed = jnp.einsum('abm,ax->bmx', env_left.astype(jnp.float32), bond_mat.astype(jnp.float32)).astype(jnp.bfloat16)
    bond_new = jnp.einsum('bma,amc->cb', mixed.astype(jnp.float32), right_f).astype(jnp.bfloat16)
    target = jnp.einsum('cbd,cx->bdx', center_new.astype(jnp.float32), bond_new.astype(jnp.float32))
    flat_target = target.reshape(chi_all * leg_width, chi_all)
    current = flat_target * (0.25 * math.sqrt(chi_all) / jnp.sqrt(jnp.sum(flat_target * flat_target)))
    for sweep_index in range(ITERS):
        gram_mat = jnp.dot(current.T, current, precision=HIGHEST)
        current = 1.5 * current - 0.5 * jnp.dot(current, gram_mat, precision=HIGHEST)
    new_left = (current * math.sqrt(chi_all * leg_width)).reshape(chi_all, leg_width, chi_all)
    return (env_new, new_left)

def reference(left_env, up_left, up_center, right_env, center, ket_tensor):
    env_list = []
    left_list = []
    for row_index in range(ROWS):
        next_index = (row_index + 1) % ROWS
        env_new, new_left = one_row(left_env[row_index], up_left[row_index], up_center[row_index], right_env[row_index], center[row_index], ket_tensor[row_index], up_left[next_index])
        env_list.append(env_new)
        left_list.append(new_left)
    return (jnp.stack(env_list), jnp.stack(left_list))
```

```python
import functools
import math

import jax
import jax.numpy as jnp
from jax import lax
from jax.experimental import pallas as pl
from jax.experimental.pallas import tpu as pltpu
from jax.sharding import PartitionSpec as P

ITERS = 5
HIGH = lax.Precision.HIGH
F32 = jnp.float32
BF16 = jnp.bfloat16
PADM = 40
MIB = 1024 * 1024


def swap(block, axis, distance):
    n = lax.axis_size(axis)
    return lax.ppermute(block, axis, [(i, i ^ distance) for i in range(n)])


def other_cell(block):
    n = lax.axis_size("cell")
    return lax.ppermute(block, "cell", [(i, (i + n - 1) % n) for i in range(n)])


GROUP = 8
LANES = GROUP * 128


def form_x(order, env_ref, up_refs, xw, count):
    width = up_refs[0].shape[1]
    unroll = 9 if count < 32 else 6

    def step(s, carry):
        for i in range(unroll):
            t = s * unroll + i
            if order is None:
                lhs = env_ref[...]
            else:
                lhs = jnp.concatenate(
                    [
                        env_ref[:, pl.ds(pl.multiple_of((order ^ d) * width, width), width)]
                        for d in range(len(up_refs))
                    ],
                    axis=1,
                )
            rhs = jnp.concatenate([ref[t] for ref in up_refs], axis=0)
            x = jnp.dot(lhs, rhs, preferred_element_type=F32)
            for b in range(count):
                rows = x[b * PADM : (b + 1) * PADM]
                g = b % GROUP
                xw[b // GROUP, t, :, g * 128 : (g + 1) * 128] = jnp.concatenate(
                    [rows[:, :128], rows[:, 128:]], axis=0
                ).astype(BF16)
        return carry

    lax.fori_loop(0, up_refs[0].shape[0] // unroll, step, 0)


def apply_site(w1_ref, w2_ref, xw, hs, y_ref, count):
    def group(p, carry):
        rows = pl.ds(pl.multiple_of(p * PADM * GROUP, PADM * GROUP), PADM * GROUP)
        for vp in range(3):
            both = []
            for v in (2 * vp, 2 * vp + 1):
                x = xw[p, 3 * v : 3 * v + 3].reshape(6 * PADM, LANES)
                both.append(jnp.dot(w1_ref[...], x, preferred_element_type=F32))
            for k in range(6):
                hs[k, vp * 144 : (vp + 1) * 144, :] = jnp.concatenate(
                    [h[k * 72 : (k + 1) * 72] for h in both], axis=0
                ).astype(BF16)
        for k in range(6):
            y = jnp.dot(w2_ref[...], hs[k], preferred_element_type=F32)
            for l in range(6):
                part = y[l * PADM : (l + 1) * PADM]
                m = k * 6 + l
                y_ref[rows, m * 128 : (m + 1) * 128] = jnp.concatenate(
                    [part[:, g * 128 : (g + 1) * 128] for g in range(GROUP)], axis=0
                ).astype(BF16)
        return carry

    lax.fori_loop(0, count // GROUP, group, 0)


def center_kernel(
    count, env_ref, u0, u1, u2, u3, w1_ref, w2_ref, re_ref, o0, o1, o2, o3, xw, hs, yc
):
    me = lax.axis_index("chi")
    z = lax.axis_index("dl")
    form_x(me, env_ref, (u0, u1, u2, u3), xw, count)
    apply_site(w1_ref, w2_ref, xw, hs, yc, count)
    result = jnp.dot(yc[...], re_ref[...], preferred_element_type=F32).astype(BF16)
    owner = pl.program_id(0) ^ z
    for d, out in enumerate((o0, o1, o2, o3)):

        @pl.when(owner == d)
        def _(out=out):
            out[...] = result


def left_kernel(
    count, first, last, env_ref, up_ref, w1_ref, w2_ref, bra_ref, *rest
):
    rest = list(rest)
    before = None if first else rest.pop(0)
    outs = [rest.pop(0) for _ in range(4 if last else 1)]
    xw, hs, yl, acc, sem_in, sem_out = rest
    me = lax.axis_index("chi")
    step = pl.program_id(0)
    steps = pl.num_programs(0)

    if not first:

        @pl.when(step == 0)
        def _():
            pltpu.make_async_copy(before, acc, sem_in).start()

    form_x(None, env_ref, [up_ref.at[i] for i in range(up_ref.shape[0])], xw, count)
    apply_site(w1_ref, w2_ref, xw, hs, yl, count)

    if not first:

        @pl.when(step == 0)
        def _():
            pltpu.make_async_copy(before, acc, sem_in).wait()

    size = 768
    chunks = yl.shape[1] // size

    def save(n):
        cols = pl.ds(pl.multiple_of(n * size, size), size)
        return pltpu.make_async_copy(acc.at[:, cols], outs[0].at[:, cols], sem_out.at[n])

    def chunk(n, carry):
        cols = pl.ds(pl.multiple_of(n * size, size), size)
        part = jnp.dot(bra_ref[...], yl[:, cols], preferred_element_type=F32)
        if first:

            @pl.when(step == 0)
            def _():
                acc[:, cols] = part

            @pl.when(step > 0)
            def _():
                acc[:, cols] += part
        else:
            acc[:, cols] += part
        if not last:

            @pl.when(step == steps - 1)
            def _():
                save(n).start()

        return carry

    lax.fori_loop(0, chunks, chunk, 0)

    @pl.when(step == steps - 1)
    def _():
        if last:
            width = acc.shape[0] // 4
            for d, out in enumerate(outs):
                rows = pl.ds(pl.multiple_of((me ^ d) * width, width), width)
                out[...] = acc[rows, :].astype(out.dtype)
        else:
            for n in range(chunks):
                save(n).wait()


def whole_spec(shape):
    zeros = (0,) * len(shape)
    return pl.BlockSpec(shape, lambda i: zeros, pipeline_mode=pl.Buffered(1))


def cost(amount):
    return pl.CostEstimate(
        flops=int(amount * 0.8e9), bytes_accessed=20 * MIB, transcendentals=0
    )


def run_center(env_rows, ups, w1, w2, re_flat, start, amount):
    count = amount // 4
    block = count * PADM
    wide = re_flat.shape[1]
    return pl.pallas_call(
        functools.partial(center_kernel, count),
        grid=(amount // count,),
        out_shape=[jax.ShapeDtypeStruct((block, wide), BF16)] * 4,
        in_specs=[pl.BlockSpec((block, env_rows.shape[1]), lambda i: (i + start // count, 0))]
        + [whole_spec(u.shape) for u in ups]
        + [whole_spec(w1.shape), whole_spec(w2.shape), whole_spec(re_flat.shape)],
        out_specs=[whole_spec((block, wide))] * 4,
        scratch_shapes=[
            pltpu.VMEM((count // GROUP, 18, 2 * PADM, LANES), BF16),
            pltpu.VMEM((6, 432, LANES), BF16),
            pltpu.VMEM((block, 36 * 128), BF16),
        ],
        compiler_params=pltpu.CompilerParams(vmem_limit_bytes=58 * MIB),
        cost_estimate=cost(amount),
        name="center_path",
    )(env_rows, *ups, w1, w2, re_flat)


def run_left(env_rows, ups, w1, w2, bra, before, start, amount, last):
    count = 32
    block = count * PADM
    chi_all = env_rows.shape[1]
    wide = 36 * 128
    first = before is None
    in_specs = (
        [pl.BlockSpec((block, chi_all), lambda i: (i + start // count, 0))]
        + [whole_spec(ups.shape), whole_spec(w1.shape), whole_spec(w2.shape)]
        + [pl.BlockSpec((bra.shape[0], block), lambda i: (0, i + start // count))]
    )
    args = [env_rows, ups, w1, w2, bra]
    if not first:
        in_specs.append(pl.BlockSpec(memory_space=pl.ANY))
        args.append(before)
    if last:
        piece = (chi_all // 4, wide)
        out_shape = [jax.ShapeDtypeStruct(piece, F32 if d == 0 else BF16) for d in range(4)]
        out_specs = [whole_spec(piece)] * 4
    else:
        out_shape = jax.ShapeDtypeStruct((chi_all, wide), F32)
        out_specs = pl.BlockSpec(memory_space=pl.ANY)
    return pl.pallas_call(
        functools.partial(left_kernel, count, first, last),
        grid=(amount // count,),
        out_shape=out_shape,
        in_specs=in_specs,
        out_specs=out_specs,
        scratch_shapes=[
            pltpu.VMEM((count // GROUP, 18, 2 * PADM, LANES), BF16),
            pltpu.VMEM((6, 432, LANES), BF16),
            pltpu.VMEM((block, wide), BF16),
            pltpu.VMEM((chi_all, wide), F32),
            pltpu.SemaphoreType.DMA,
            pltpu.SemaphoreType.DMA((wide // 768,)),
        ],
        compiler_params=pltpu.CompilerParams(vmem_limit_bytes=60 * MIB),
        cost_estimate=cost(amount),
        name="left_path",
    )(*args)


def place_kernel(p0, p1, p2, p3, out_ref):
    z = lax.axis_index("dl")
    rows, legs, _ = out_ref.shape
    own = rows // 8
    for d, ref in enumerate((p0, p1, p2, p3)):
        for n in range(0, 2 * own, 2):
            pair = ref[n * PADM : (n + 2) * PADM, :].astype(F32)
            base = n // own * (rows // 2) + (z ^ d) * own + n % own
            out_ref[base] = pair[:legs]
            out_ref[base + 1] = pair[PADM : PADM + legs]


def run_place(parts, rows, legs):
    cols = parts[0].shape[1]
    return pl.pallas_call(
        place_kernel,
        out_shape=jax.ShapeDtypeStruct((rows, legs, cols), F32),
        compiler_params=pltpu.CompilerParams(vmem_limit_bytes=32 * MIB),
        name="place_rows",
    )(*parts)


def one_hot(rows, cols, row_of, col_of):
    r = lax.broadcasted_iota(jnp.int32, (rows, cols), 0)
    c = lax.broadcasted_iota(jnp.int32, (rows, cols), 1)
    return row_of(r) == col_of(c)


def site_matrices(ket):
    g, phys = ket.shape[0], ket.shape[4]
    two, wp = g * g, g * phys
    tall, wide = two * wp, g * PADM

    def spread(mat, left, right, keep):
        rows = jnp.dot(left.astype(BF16), mat, preferred_element_type=F32).astype(BF16)
        full = jnp.dot(rows, right.astype(BF16), preferred_element_type=F32)
        return jnp.where(keep, full, 0.0).astype(BF16)

    def same(n):
        return n

    one = jnp.transpose(ket, (2, 3, 4, 1, 0)).reshape(two * phys, two)
    w1 = spread(
        one,
        one_hot(tall, two * phys, lambda n: n // (g * wp) * wp + n % wp, same),
        one_hot(two, wide, same, lambda q: jnp.where(q % PADM < two, q // PADM * g + q % PADM // g, -1)),
        one_hot(tall, wide, lambda n: n // wp % g, lambda q: q % PADM % g),
    )
    other = jnp.transpose(ket, (2, 3, 1, 0, 4)).reshape(two, two * phys)
    w2 = spread(
        other,
        one_hot(wide, two, lambda n: jnp.where(n % PADM < two, n // PADM * g + n % PADM % g, -1), same),
        one_hot(two * phys, tall, same, lambda q: q // wp * phys + q % phys),
        one_hot(wide, tall, lambda n: n % PADM // g, lambda q: q % wp // phys),
    )
    return w1, w2


def up_pairs(up):
    a, two, c = up.shape
    x = up.reshape(a, 3, 2, 6, c)
    x = jnp.transpose(x, (3, 1, 0, 2, 4))
    return x.reshape(18, a, 2 * c)


def fast(left_env, up_left, up_center, right_env, center, ket_tensor):
    env_local = left_env[0]
    left_iso = up_left[0]
    left_mid = up_center[0]
    env_right = right_env[0]
    bond_mat = center[0]
    site_ket = ket_tensor[0]
    chi_all, rows, leg_width = env_local.shape
    cols = left_iso.shape[2]
    z = lax.axis_index("dl")
    me = lax.axis_index("chi")
    after = lax.optimization_barrier

    def add_up(parts):
        total = parts[0].astype(F32)
        for part in parts[1:]:
            total = total + part.astype(F32)
        return total

    bra = jnp.pad(left_iso, ((0, 0), (0, PADM - leg_width), (0, 0)))
    bra = other_cell(bra.reshape(rows * PADM, cols).T)
    mid = up_pairs(left_mid)
    env_local, env_right, left_iso, site_ket, bra, mid = after((env_local, env_right, left_iso, site_ket, bra, mid))
    bra_all = lax.all_gather(bra, "dl", axis=0, tiled=True)
    mids = [mid] + [swap(mid, "chi", d) for d in (1, 2, 3)]
    w1, w2 = site_matrices(site_ket)
    env_rows = jnp.pad(
        jnp.transpose(env_local, (1, 2, 0)), ((0, 0), (0, PADM - leg_width), (0, 0))
    ).reshape(rows * PADM, chi_all)
    re_flat = jnp.transpose(env_right, (1, 0, 2)).reshape(leg_width * cols, chi_all)
    mixed = jnp.dot(env_rows, bond_mat, preferred_element_type=F32).astype(BF16)
    mixed = mixed.reshape(rows, PADM, cols)[:, :leg_width].reshape(rows, leg_width * cols)
    bond = jnp.dot(mixed, re_flat, preferred_element_type=F32)
    iso = up_pairs(left_iso)

    w1, w2, iso, bond, env_rows, *mids = after((w1, w2, iso, bond, env_rows, *mids))
    bond_in = swap(bond, "dl", 1)
    half = rows // 2
    terms_a = run_center(env_rows, mids, w1, w2, re_flat, 0, half)

    bond, bond_in, bra_all, iso, *terms_a = after((bond, bond_in, bra_all, iso, *terms_a))
    isos = lax.all_gather(iso, "chi", axis=0)
    bond = bond + bond_in
    got_a = [terms_a[0]] + [swap(terms_a[d], "dl", d) for d in (1, 2, 3)]
    bond_in = swap(bond, "dl", 2)
    env_rows, bond, *mids = after((env_rows, bond, *mids))
    terms_b = run_center(env_rows, mids, w1, w2, re_flat, half, half)

    bond, bond_in, env_rows, *both = after((bond, bond_in, env_rows, *terms_b, *got_a))
    terms_b, got_a = both[:4], both[4:]
    bond = (bond + bond_in).astype(BF16)
    got_b = [terms_b[0]] + [swap(terms_b[d], "dl", d) for d in (1, 2, 3)]
    bond_in = swap(bond, "chi", 1)
    own_a = add_up(got_a).astype(BF16)
    env_rows, bond, own_a = after((env_rows, bond, own_a))
    acc = run_left(env_rows, isos, w1, w2, bra_all, None, 0, half, False)

    acc, bond, bond_in, *got_b = after((acc, bond, bond_in, *got_b))
    own_center = jnp.concatenate([own_a, add_up(got_b).astype(BF16)], axis=0)
    cross = lax.dot_general(
        own_center, own_center, (((0,), (0,)), ((), ())), preferred_element_type=F32
    )
    crosses = [lax.dynamic_slice_in_dim(cross, (me ^ d) * rows, rows, 0) for d in range(4)]
    crosses = crosses[:1] + [swap(crosses[d], "chi", d) for d in (1, 2, 3)]
    bond = jnp.concatenate([bond, bond_in], axis=0)
    bond_in = swap(bond, "chi", 2)
    acc, cross, bond = after((acc, cross, bond))
    quarter = half // 2
    acc = run_left(env_rows, isos, w1, w2, bra_all, acc, half, quarter, False)

    acc, bond, bond_in, *crosses = after((acc, bond, bond_in, *crosses))
    cross = add_up(crosses)
    crosses = [cross] + [swap(cross, "dl", d) for d in (1, 2, 3)]
    acc, cross = after((acc, cross))
    sums = run_left(env_rows, isos, w1, w2, bra_all, acc, half + quarter, quarter, True)

    sums, crosses = list(sums), list(crosses)
    *sums, c0, c1, c2, c3 = after((*sums, *crosses))
    cross = (c0 + c1) + (c2 + c3)
    crosses = [cross] + [swap(cross, "chi", d) for d in (1, 2, 3)]
    parts = sums[:1] + [swap(sums[d], "chi", d) for d in (1, 2, 3)]

    def by_index(blocks):
        both = jnp.stack(blocks)
        return [lax.dynamic_index_in_dim(both, me ^ d, 0, False) for d in range(4)]

    cross = jnp.concatenate(by_index(crosses), axis=0)
    bond = jnp.concatenate([bond, bond_in], axis=0).reshape(4, rows, chi_all)
    bond_full = jnp.concatenate(by_index(list(bond)), axis=0)

    bond_wide = bond_full.astype(F32)
    gram = jnp.dot(jnp.dot(bond_wide, cross, precision=HIGH), bond_wide.T, precision=HIGH)
    one = jnp.eye(chi_all, dtype=F32)
    factor = 0.25 * math.sqrt(chi_all) / jnp.sqrt(jnp.sum(gram * one))
    gram = gram * (factor * factor)
    product = None
    for sweep_index in range(ITERS):
        step = 1.5 * one - 0.5 * gram
        product = step if product is None else jnp.dot(product, step, precision=HIGH)
        if sweep_index < ITERS - 1:
            gram = jnp.dot(jnp.dot(step, gram, precision=HIGH), step, precision=HIGH)
    weight = lax.dot_general(bond_wide, product, (((0,), (0,)), ((), ())), precision=HIGH)
    weight = (weight * (factor * math.sqrt(chi_all * leg_width))).astype(BF16)
    pieces = []
    for d in (3, 2, 1, 0):
        mine = lax.dynamic_slice_in_dim(weight, (z ^ d) * cols, cols, 1)
        part = jnp.dot(own_center, mine, preferred_element_type=F32).astype(BF16)
        pieces.append(swap(part, "dl", d) if d > 0 else part)
    new_left = run_place(pieces[::-1], rows, leg_width)
    env_new = add_up(parts).reshape(rows, leg_width, cols)
    return (env_new[None], new_left[None])


def from_behind(block, axis, distance):
    devices = range(lax.axis_size(axis))
    route = [((i - distance) % len(devices), i) for i in devices]
    return lax.ppermute(block, axis, route)


def pick(rows, cols, row_of, col_of):
    r = lax.broadcasted_iota(jnp.int32, (rows, cols), 0)
    c = lax.broadcasted_iota(jnp.int32, (rows, cols), 1)
    return (row_of(r) == col_of(c)).astype(BF16)


def double_layer(tensor, pad):
    leg = tensor.shape[0]
    two = leg * leg
    phys = tensor.shape[4]
    big = two * pad

    def outer(first):
        def code(n):
            m, s = n // pad, n % pad
            a = m // leg if first else m % leg
            b = s // leg if first else s % leg
            return jnp.where(s < two, a * leg + b, -1)

        return code

    def same(n):
        return n

    total = None
    ket_rows = pick(big, two, outer(True), same)
    bra_rows = pick(big, two, outer(False), same)
    for p in range(phys):
        mat = tensor[:, :, :, :, p].reshape(two, two)
        ket_small = jnp.dot(ket_rows, mat, preferred_element_type=F32).astype(BF16)
        bra_small = jnp.dot(bra_rows, mat, preferred_element_type=F32).astype(BF16)
        ket = lax.dot_general(ket_small, ket_rows, (((1,), (1,)), ((), ())), preferred_element_type=F32)
        bra = lax.dot_general(bra_small, bra_rows, (((1,), (1,)), ((), ())), preferred_element_type=F32)
        total = ket * bra if total is None else total + ket * bra
    return total.astype(BF16)


def through_site(env, stacked, layer, pad):
    two = env.shape[2]
    summed = jnp.einsum("abm,asc->bmsc", env, stacked, preferred_element_type=F32).astype(BF16)
    amount, columns = summed.shape[0], summed.shape[3]
    flat = summed.reshape(amount, two * pad, columns)
    out = jnp.einsum("tn,btc->bnc", layer, flat, preferred_element_type=F32).astype(BF16)
    return out.reshape(amount, two, pad, columns)


def shards(left_env, up_left, up_center, right_env, center, ket_tensor):
    env_local = left_env[0]
    left_iso = up_left[0]
    left_mid = up_center[0]
    env_right = right_env[0]
    bond_mat = center[0]
    site_ket = ket_tensor[0]
    chi_all = env_local.shape[0]
    leg_width = env_local.shape[2]
    pad = -(-leg_width // 8) * 8
    widen = ((0, 0), (0, pad - leg_width), (0, 0))
    rows = left_iso.shape[0]
    col_count = left_iso.shape[2]

    mid_all = lax.all_gather(left_mid, "chi", axis=0, tiled=True)
    iso_all = lax.all_gather(left_iso, "chi", axis=0, tiled=True)
    next_iso = from_behind(left_iso, "cell", -1)
    bra_iso = lax.all_gather(next_iso, "dl", axis=2, tiled=True)

    layer = double_layer(site_ket, pad)

    mixed = jnp.einsum("abm,ax->bmx", env_local, bond_mat, preferred_element_type=F32).astype(BF16)
    bond_term = jnp.einsum("bma,amc->bc", mixed, env_right, preferred_element_type=F32)
    bond_slots = lax.dynamic_update_slice(
        jnp.zeros((chi_all, chi_all), F32), bond_term, (lax.axis_index("chi") * rows, 0)
    )
    bond_full = lax.psum(bond_slots, ("chi", "dl")).astype(BF16)

    right_cut = through_site(env_local, jnp.pad(mid_all, widen), layer, pad)
    center_term = jnp.einsum(
        "bmda,amc->bdc", right_cut[:, :, :leg_width], env_right, preferred_element_type=F32
    ).astype(BF16)
    iso_all, center_term = lax.optimization_barrier((iso_all, center_term))
    center_part = lax.psum_scatter(center_term, "dl", scatter_dimension=0, tiled=True)
    cross = lax.psum(
        jnp.einsum("bdc,bdy->cy", center_part, center_part, preferred_element_type=F32),
        ("chi", "dl"),
    )
    center_all = lax.all_gather(center_part, "dl", axis=0, tiled=True)

    left_cut = through_site(env_local, jnp.pad(iso_all, widen), layer, pad)
    env_term = jnp.einsum(
        "bmdc,bdk->kmc", left_cut[:, :, :leg_width], bra_iso, preferred_element_type=F32
    ).astype(BF16)
    env_new = lax.psum_scatter(env_term, "chi", scatter_dimension=0, tiled=True).astype(F32)

    bond_wide = bond_full.astype(F32)
    gram = jnp.dot(
        jnp.dot(bond_wide, cross, precision=HIGH), bond_wide.T, precision=HIGH
    )
    one = jnp.eye(chi_all, dtype=F32)
    norm_sum = jnp.sum(gram * one)
    factor = 0.25 * math.sqrt(chi_all) / jnp.sqrt(norm_sum)
    gram = gram * (factor * factor)
    product = None
    for sweep_index in range(ITERS):
        step = 1.5 * one - 0.5 * gram
        product = step if product is None else jnp.dot(product, step, precision=HIGH)
        if sweep_index < ITERS - 1:
            gram = jnp.dot(jnp.dot(step, gram, precision=HIGH), step, precision=HIGH)
    mine = lax.dynamic_slice_in_dim(product, lax.axis_index("dl") * col_count, col_count, 1)
    weight = lax.dot_general(bond_wide, mine, (((0,), (0,)), ((), ())), precision=HIGH)
    weight = weight * (factor * math.sqrt(chi_all * leg_width))
    new_left = jnp.einsum("bdc,cx->bdx", center_all.astype(F32), weight, precision=HIGH)
    return (env_new[None], new_left[None])


def solution(mesh):
    placed = (
        P("cell", None, "chi", None),
        P("cell", "chi", None, "dl"),
        P("cell", "chi", None, "dl"),
        P("cell", "dl", None, None),
        P("cell", None, "dl"),
        P("cell", None, None, None, None, None),
    )
    fits = mesh.shape["chi"] == 4 and mesh.shape["dl"] == 4 and mesh.shape["cell"] == 2
    return jax.shard_map(
        fast if fits else shards,
        mesh=mesh,
        in_specs=placed,
        out_specs=(P("cell", "chi", None, "dl"), P("cell", "chi", None, "dl")),
        check_vma=False,
    )
```

```python
import functools
import math

import jax
import jax.numpy as jnp
from jax import lax
from jax.experimental import pallas as pl
from jax.experimental.pallas import tpu as pltpu
from jax.sharding import PartitionSpec as P

ITERS = 5
HIGH = lax.Precision.HIGH
F32 = jnp.float32
BF16 = jnp.bfloat16
PADM = 40
MIB = 1024 * 1024


def swap(block, axis, distance):
    n = lax.axis_size(axis)
    return lax.ppermute(block, axis, [(i, i ^ distance) for i in range(n)])


def other_cell(block):
    n = lax.axis_size("cell")
    return lax.ppermute(block, "cell", [(i, (i + n - 1) % n) for i in range(n)])


GROUP = 8
LANES = GROUP * 128


def store_x(t, lhs, rhs, xw, count):
    x = jnp.dot(lhs, rhs, preferred_element_type=F32)
    for b in range(count):
        rows = x[b * PADM : (b + 1) * PADM]
        g = b % GROUP
        xw[b // GROUP, t, :, g * 128 : (g + 1) * 128] = jnp.concatenate(
            [rows[:, :128], rows[:, 128:]], axis=0
        ).astype(BF16)


def apply_site(w1_ref, w2_ref, xw, hs, y_ref, count):
    def group(p, carry):
        rows = pl.ds(pl.multiple_of(p * PADM * GROUP, PADM * GROUP), PADM * GROUP)
        for vp in range(3):
            both = []
            for v in (2 * vp, 2 * vp + 1):
                x = xw[p, 3 * v : 3 * v + 3].reshape(6 * PADM, LANES)
                both.append(jnp.dot(w1_ref[...], x, preferred_element_type=F32))
            for k in range(6):
                hs[k, vp * 144 : (vp + 1) * 144, :] = jnp.concatenate(
                    [h[k * 72 : (k + 1) * 72] for h in both], axis=0
                ).astype(BF16)
        for k in range(6):
            y = jnp.dot(w2_ref[...], hs[k], preferred_element_type=F32)
            for l in range(6):
                part = y[l * PADM : (l + 1) * PADM]
                m = k * 6 + l
                y_ref[rows, m * 128 : (m + 1) * 128] = jnp.concatenate(
                    [part[:, g * 128 : (g + 1) * 128] for g in range(GROUP)], axis=0
                ).astype(BF16)
        return carry

    lax.fori_loop(0, count // GROUP, group, 0)


def center_kernel(
    count, env_ref, u0, u1, u2, u3, u4, w1_ref, w2_ref, re_ref, o0, o1, o2, o3, xw, hs, yc
):
    me = lax.axis_index("chi")
    z = lax.axis_index("dl")
    width = u0.shape[1]
    cut = u3.shape[0]

    def column(leg):
        far = u3[leg] if leg < cut else u4[leg - cut]
        return jnp.concatenate([u0[leg], u1[leg], u2[leg], far], axis=0)

    for t in range(u0.shape[0] // 2):
        lhs = jnp.concatenate(
            [
                env_ref[:, pl.ds(pl.multiple_of((me ^ d) * width, width), width)]
                for d in range(4)
            ],
            axis=1,
        )
        leg = t % 3 * 12 + t // 3
        rhs = jnp.concatenate([column(leg), column(leg + 6)], axis=1)
        store_x(t, lhs, rhs, xw, count)
    apply_site(w1_ref, w2_ref, xw, hs, yc, count)
    result = jnp.dot(yc[...], re_ref[...], preferred_element_type=F32).astype(BF16)
    owner = pl.program_id(0) ^ z
    for d, out in enumerate((o0, o1, o2, o3)):

        @pl.when(owner == d)
        def _(out=out):
            out[...] = result


def left_kernel(
    count, first, last, env_ref, up_ref, w1_ref, w2_ref, bra_ref, *rest
):
    rest = list(rest)
    before = None if first else rest.pop(0)
    outs = [rest.pop(0) for _ in range(7 if last else 1)]
    xw, hs, yl, acc, sem_in, sem_out = rest
    me = lax.axis_index("chi")
    step = pl.program_id(0)
    steps = pl.num_programs(0)

    if not first:

        @pl.when(step == 0)
        def _():
            pltpu.make_async_copy(before, acc, sem_in).start()

    unroll = 6

    def form(s, carry):
        for i in range(unroll):
            leg = i % 3 * 12 + s * (unroll // 3) + i // 3
            rhs = jnp.concatenate(
                [
                    jnp.concatenate([up_ref[d, leg + n] for d in range(up_ref.shape[0])], axis=0)
                    for n in (0, 6)
                ],
                axis=1,
            )
            store_x(s * unroll + i, env_ref[...], rhs, xw, count)
        return carry

    lax.fori_loop(0, up_ref.shape[1] // (2 * unroll), form, 0)
    apply_site(w1_ref, w2_ref, xw, hs, yl, count)

    if not first:

        @pl.when(step == 0)
        def _():
            pltpu.make_async_copy(before, acc, sem_in).wait()

    size = 768
    chunks = yl.shape[1] // size

    def save(n):
        cols = pl.ds(pl.multiple_of(n * size, size), size)
        return pltpu.make_async_copy(acc.at[:, cols], outs[0].at[:, cols], sem_out.at[n])

    def chunk(n, carry):
        cols = pl.ds(pl.multiple_of(n * size, size), size)
        part = jnp.dot(bra_ref[...], yl[:, cols], preferred_element_type=F32)
        if first:

            @pl.when(step == 0)
            def _():
                acc[:, cols] = part

            @pl.when(step > 0)
            def _():
                acc[:, cols] += part
        else:
            acc[:, cols] += part
        if not last:

            @pl.when(step == steps - 1)
            def _():
                save(n).start()

        return carry

    lax.fori_loop(0, chunks, chunk, 0)

    @pl.when(step == steps - 1)
    def _():
        if last:
            width = acc.shape[0] // 8
            outs[0][...] = acc[pl.ds(pl.multiple_of(me * 2 * width, 2 * width), 2 * width), :]
            for n, out in enumerate(outs[1:]):
                place = ((me ^ (n // 2 + 1)) * 2 + n % 2) * width
                rows = pl.ds(pl.multiple_of(place, width), width)
                out[...] = acc[rows, :].astype(out.dtype)
        else:
            for n in range(chunks):
                save(n).wait()


def whole_spec(shape):
    zeros = (0,) * len(shape)
    return pl.BlockSpec(shape, lambda i: zeros, pipeline_mode=pl.Buffered(1))


def cost(amount):
    return pl.CostEstimate(
        flops=int(amount * 0.8e9), bytes_accessed=20 * MIB, transcendentals=0
    )


def run_center(env_rows, ups, w1, w2, re_flat, start, amount):
    count = amount // 4
    block = count * PADM
    wide = re_flat.shape[1]
    return pl.pallas_call(
        functools.partial(center_kernel, count),
        grid=(amount // count,),
        out_shape=[jax.ShapeDtypeStruct((block, wide), BF16)] * 4,
        in_specs=[pl.BlockSpec((block, env_rows.shape[1]), lambda i: (i + start // count, 0))]
        + [whole_spec(u.shape) for u in ups]
        + [whole_spec(w1.shape), whole_spec(w2.shape), whole_spec(re_flat.shape)],
        out_specs=[whole_spec((block, wide))] * 4,
        scratch_shapes=[
            pltpu.VMEM((count // GROUP, 18, 2 * PADM, LANES), BF16),
            pltpu.VMEM((6, 432, LANES), BF16),
            pltpu.VMEM((block, 36 * 128), BF16),
        ],
        compiler_params=pltpu.CompilerParams(vmem_limit_bytes=58 * MIB),
        cost_estimate=cost(amount),
        name="center_path",
    )(env_rows, *ups, w1, w2, re_flat)


def run_left(env_rows, ups, w1, w2, bra, before, start, amount, last):
    count = 32
    block = count * PADM
    chi_all = env_rows.shape[1]
    wide = 36 * 128
    first = before is None
    in_specs = (
        [pl.BlockSpec((block, chi_all), lambda i: (i + start // count, 0))]
        + [whole_spec(ups.shape), whole_spec(w1.shape), whole_spec(w2.shape)]
        + [pl.BlockSpec((bra.shape[0], block), lambda i: (0, i + start // count))]
    )
    args = [env_rows, ups, w1, w2, bra]
    if not first:
        in_specs.append(pl.BlockSpec(memory_space=pl.ANY))
        args.append(before)
    if last:
        own, piece = (chi_all // 4, wide), (chi_all // 8, wide)
        out_shape = [jax.ShapeDtypeStruct(own, F32)] + [jax.ShapeDtypeStruct(piece, BF16)] * 6
        out_specs = [whole_spec(own)] + [whole_spec(piece)] * 6
    else:
        out_shape = jax.ShapeDtypeStruct((chi_all, wide), F32)
        out_specs = pl.BlockSpec(memory_space=pl.ANY)
    return pl.pallas_call(
        functools.partial(left_kernel, count, first, last),
        grid=(amount // count,),
        out_shape=out_shape,
        in_specs=in_specs,
        out_specs=out_specs,
        scratch_shapes=[
            pltpu.VMEM((count // GROUP, 18, 2 * PADM, LANES), BF16),
            pltpu.VMEM((6, 432, LANES), BF16),
            pltpu.VMEM((block, wide), BF16),
            pltpu.VMEM((chi_all, wide), F32),
            pltpu.SemaphoreType.DMA,
            pltpu.SemaphoreType.DMA((wide // 768,)),
        ],
        compiler_params=pltpu.CompilerParams(vmem_limit_bytes=60 * MIB),
        cost_estimate=cost(amount),
        name="left_path",
    )(*args)


def split(x):
    high = x.astype(BF16)
    return high, (x - high.astype(F32)).astype(BF16)


def product_of(a, b):
    (ah, al), (bh, bl) = split(a), split(b)
    small = jnp.dot(ah, bl, preferred_element_type=F32) + jnp.dot(
        al, bh, preferred_element_type=F32
    )
    return small + jnp.dot(ah, bh, preferred_element_type=F32)


def polar_kernel(scale, bond_ref, cross_ref, center_ref, p0, p1, p2, p3, hold):
    n = bond_ref.shape[0]
    cols = p0.shape[1]
    z = lax.axis_index("dl")
    bond = bond_ref[...]
    turned = (((1,), (1,)), ((), ()))
    high, low = split(cross_ref[...])
    half = jnp.dot(bond, high, preferred_element_type=F32) + jnp.dot(
        bond, low, preferred_element_type=F32
    )
    high, low = split(half)
    half = lax.dot_general(high, bond, turned, preferred_element_type=F32) + lax.dot_general(
        low, bond, turned, preferred_element_type=F32
    )
    gram = half + half.T
    same = lax.broadcasted_iota(jnp.int32, (n, n), 0) == lax.broadcasted_iota(
        jnp.int32, (n, n), 1
    )
    trace = jnp.sum(jnp.where(same, gram, 0.0), axis=1, keepdims=True)
    trace = jnp.sum(trace, axis=0, keepdims=True)
    factor = 0.25 * math.sqrt(n) / jnp.sqrt(trace)
    gram = gram * (factor * factor)
    diagonal = jnp.where(same, 1.5, 0.0)
    result = None
    for sweep_index in range(ITERS):
        step = diagonal - 0.5 * gram
        result = step if result is None else product_of(result, step)
        if sweep_index < ITERS - 1:
            gram = product_of(product_of(step, gram), step)
    hold[...] = result
    high, low = split(
        jnp.concatenate(
            [hold[:, pl.ds(pl.multiple_of((z ^ d) * cols, cols), cols)] for d in range(4)],
            axis=1,
        )
    )
    inner = (((0,), (0,)), ((), ()))
    weight = lax.dot_general(bond, high, inner, preferred_element_type=F32)
    weight = weight + lax.dot_general(bond, low, inner, preferred_element_type=F32)
    weight = (weight * (factor * scale)).astype(BF16)
    y = jnp.dot(center_ref[...], weight, preferred_element_type=F32).astype(BF16)
    for d, out in enumerate((p0, p1, p2, p3)):
        out[...] = y[:, d * cols : (d + 1) * cols]


def run_polar(bond, cross, center, scale, cols):
    n = bond.shape[0]
    return pl.pallas_call(
        functools.partial(polar_kernel, scale),
        out_shape=[jax.ShapeDtypeStruct((center.shape[0], cols), BF16)] * 4,
        scratch_shapes=[pltpu.VMEM((n, n), F32)],
        compiler_params=pltpu.CompilerParams(vmem_limit_bytes=58 * MIB),
        cost_estimate=pl.CostEstimate(flops=1000, bytes_accessed=1000, transcendentals=0),
        name="polar",
    )(bond, cross, center)


def place_kernel(p0, p1, p2, p3, out_ref):
    z = lax.axis_index("dl")
    legs, rows, _ = out_ref.shape
    own = rows // 8
    for d, ref in enumerate((p0, p1, p2, p3)):
        for n in range(0, 2 * own, 2):
            pair = ref[n * PADM : (n + 2) * PADM, :].astype(F32)
            row = n // own * (rows // 2) + (z ^ d) * own + n % own
            out_ref[:, row, :] = pair[:legs]
            out_ref[:, row + 1, :] = pair[PADM : PADM + legs]


def run_place(parts, rows, legs):
    return pl.pallas_call(
        place_kernel,
        out_shape=jax.ShapeDtypeStruct((legs, rows, parts[0].shape[1]), F32),
        compiler_params=pltpu.CompilerParams(vmem_limit_bytes=58 * MIB),
        name="new_rows",
    )(*parts)


def env_kernel(own_ref, a1, a2, b1, b2, out_ref):
    cols = out_ref.shape[2]

    def add(one, two):
        for m in range(out_ref.shape[0]):
            lanes = slice(m * cols, (m + 1) * cols)
            part = one[:, lanes].astype(F32) + two[:, lanes].astype(F32)
            out_ref[m] = own_ref[:, lanes] + part

    @pl.when(pl.program_id(0) < 2)
    def _():
        add(a1, a2)

    @pl.when(pl.program_id(0) >= 2)
    def _():
        add(b1, b2)


def run_env(own, a1, a2, b1, b2, legs):
    rows, wide = own.shape
    size = rows // 4
    low = pl.BlockSpec((size, wide), lambda i: (jnp.minimum(i, 1), 0))
    high = pl.BlockSpec((size, wide), lambda i: (jnp.maximum(i - 2, 0), 0))
    return pl.pallas_call(
        env_kernel,
        grid=(4,),
        out_shape=jax.ShapeDtypeStruct((legs, rows, wide // legs), F32),
        in_specs=[pl.BlockSpec((size, wide), lambda i: (i, 0)), low, low, high, high],
        out_specs=pl.BlockSpec((legs, size, wide // legs), lambda i: (0, i, 0)),
        compiler_params=pltpu.CompilerParams(vmem_limit_bytes=58 * MIB),
        name="new_env",
    )(own, a1, a2, b1, b2)


def one_hot(rows, cols, row_of, col_of):
    r = lax.broadcasted_iota(jnp.int32, (rows, cols), 0)
    c = lax.broadcasted_iota(jnp.int32, (rows, cols), 1)
    return row_of(r) == col_of(c)


def site_matrices(ket):
    g, phys = ket.shape[0], ket.shape[4]
    two, wp = g * g, g * phys
    tall, wide = two * wp, g * PADM

    def spread(mat, left, right, keep):
        rows = jnp.dot(left.astype(BF16), mat, preferred_element_type=F32).astype(BF16)
        full = jnp.dot(rows, right.astype(BF16), preferred_element_type=F32)
        return jnp.where(keep, full, 0.0).astype(BF16)

    def same(n):
        return n

    one = jnp.transpose(ket, (2, 3, 4, 1, 0)).reshape(two * phys, two)
    w1 = spread(
        one,
        one_hot(tall, two * phys, lambda n: n // (g * wp) * wp + n % wp, same),
        one_hot(two, wide, same, lambda q: jnp.where(q % PADM < two, q // PADM * g + q % PADM // g, -1)),
        one_hot(tall, wide, lambda n: n // wp % g, lambda q: q % PADM % g),
    )
    other = jnp.transpose(ket, (2, 3, 1, 0, 4)).reshape(two, two * phys)
    w2 = spread(
        other,
        one_hot(wide, two, lambda n: jnp.where(n % PADM < two, n // PADM * g + n % PADM % g, -1), same),
        one_hot(two * phys, tall, same, lambda q: q // wp * phys + q % phys),
        one_hot(wide, tall, lambda n: n % PADM // g, lambda q: q % wp // phys),
    )
    return w1, w2


def fast(left_env, up_left, up_center, right_env, center, ket_tensor):
    env_local = left_env[0]
    left_iso = up_left[0]
    left_mid = up_center[0]
    env_right = right_env[0]
    bond_mat = center[0]
    site_ket = ket_tensor[0]
    chi_all, rows, leg_width = env_local.shape
    cols = left_iso.shape[2]
    z = lax.axis_index("dl")
    me = lax.axis_index("chi")
    after = lax.optimization_barrier

    def add_up(parts):
        total = parts[0].astype(F32)
        for part in parts[1:]:
            total = total + part.astype(F32)
        return total

    bra = jnp.pad(left_iso, ((0, 0), (0, PADM - leg_width), (0, 0)))
    bra = other_cell(bra.reshape(rows * PADM, cols).T)
    mid = jnp.transpose(left_mid, (1, 0, 2))
    env_local, env_right, left_iso, site_ket, bra, mid = after((env_local, env_right, left_iso, site_ket, bra, mid))
    bra_all = lax.all_gather(bra, "dl", axis=0, tiled=True)
    mid1, mid2 = swap(mid, "chi", 1), swap(mid, "chi", 2)
    cut = mid.shape[0] // 2
    far_a, far_b = swap(mid2[:cut], "chi", 1), swap(mid1[cut:], "chi", 2)
    mids = [mid, mid1, mid2, far_a, far_b]
    w1, w2 = site_matrices(site_ket)
    env_rows = jnp.pad(
        jnp.transpose(env_local, (1, 2, 0)), ((0, 0), (0, PADM - leg_width), (0, 0))
    ).reshape(rows * PADM, chi_all)
    re_flat = jnp.transpose(env_right, (1, 0, 2)).reshape(leg_width * cols, chi_all)
    mixed = jnp.dot(env_rows, bond_mat, preferred_element_type=F32).astype(BF16)
    mixed = mixed.reshape(rows, PADM, cols)[:, :leg_width].reshape(rows, leg_width * cols)
    bond = jnp.dot(mixed, re_flat, preferred_element_type=F32)
    iso = jnp.transpose(left_iso, (1, 0, 2))

    w1, w2, iso, bond, env_rows, *mids = after((w1, w2, iso, bond, env_rows, *mids))
    bond_in = swap(bond, "dl", 1)
    half = rows // 2
    terms_a = run_center(env_rows, mids, w1, w2, re_flat, 0, half)

    bond, bond_in, bra_all, iso, *terms_a = after((bond, bond_in, bra_all, iso, *terms_a))
    isos = lax.all_gather(iso, "chi", axis=0)
    bond = bond + bond_in
    got_a = [terms_a[0]] + [swap(terms_a[d], "dl", d) for d in (1, 2, 3)]
    bond_in = swap(bond, "dl", 2)
    env_rows, bond, *mids = after((env_rows, bond, *mids))
    terms_b = run_center(env_rows, mids, w1, w2, re_flat, half, half)

    bond, bond_in, env_rows, *both = after((bond, bond_in, env_rows, *terms_b, *got_a))
    terms_b, got_a = both[:4], both[4:]
    bond = (bond + bond_in).astype(BF16)
    got_b = [terms_b[0]] + [swap(terms_b[d], "dl", d) for d in (1, 2, 3)]
    bond_in = swap(bond, "chi", 1)
    own_a = add_up(got_a).astype(BF16)
    env_rows, bond, own_a = after((env_rows, bond, own_a))
    acc = run_left(env_rows, isos, w1, w2, bra_all, None, 0, half, False)

    acc, bond, bond_in, *got_b = after((acc, bond, bond_in, *got_b))
    own_b = add_up(got_b).astype(BF16)
    own_center = jnp.concatenate([own_a, own_b], axis=0)
    cross = lax.dot_general(
        own_center, own_center, (((0,), (0,)), ((), ())), preferred_element_type=F32
    )
    def exchange(block, axis):
        block = block.astype(BF16)
        return [block] + [swap(block, axis, d) for d in (1, 2, 3)]

    def total_of(c0, c1, c2, c3):
        return (c0.astype(F32) + c1.astype(F32)) + (c2.astype(F32) + c3.astype(F32))

    upper = [cross[n * rows : (n + 1) * rows, n * rows :] for n in range(4)]
    cross = jnp.concatenate(upper, axis=1)
    crosses = exchange(cross, "chi")
    bond = jnp.concatenate([bond, bond_in], axis=0)
    bond_in = swap(bond, "chi", 2)
    acc, cross, bond = after((acc, cross, bond))
    quarter = half // 2
    acc = run_left(env_rows, isos, w1, w2, bra_all, acc, half, quarter, False)

    acc, bond, bond_in, *crosses = after((acc, bond, bond_in, *crosses))
    cross = total_of(*crosses)
    crosses = exchange(cross, "dl")
    acc, cross = after((acc, cross))
    sums = run_left(env_rows, isos, w1, w2, bra_all, acc, half + quarter, quarter, True)

    sums, crosses = list(sums), list(crosses)
    *sums, c0, c1, c2, c3 = after((*sums, *crosses))
    cross = total_of(c0, c1, c2, c3)
    own, x_a, x_b, y_a, y_b, far_a, far_b = sums
    far_a, far_b = swap(far_a, "chi", 1), swap(far_b, "chi", 2)
    x_a, y_b = swap(x_a, "chi", 1), swap(y_b, "chi", 2)

    def by_index(blocks):
        both = jnp.stack(blocks)
        return [lax.dynamic_index_in_dim(both, me ^ d, 0, False) for d in range(4)]

    blocks, start = [], 0
    for n in range(4):
        stop = start + (4 - n) * rows
        blocks.append(
            jnp.concatenate(
                [
                    jnp.zeros((rows, n * rows), F32),
                    0.5 * cross[:, start : start + rows],
                    cross[:, start + rows : stop],
                ],
                axis=1,
            )
        )
        start = stop
    cross = jnp.concatenate(blocks, axis=0)
    bond = jnp.concatenate([bond, bond_in], axis=0).reshape(4, rows, chi_all)
    bond_full = jnp.concatenate(by_index(list(bond)), axis=0)

    pieces = run_polar(
        bond_full, cross, own_center, math.sqrt(chi_all * leg_width), cols
    )
    far_a, far_b, *pieces = after((far_a, far_b, *pieces))
    pieces[3] = swap(pieces[3], "dl", 3)
    x_b = swap((x_b.astype(F32) + far_b.astype(F32)).astype(BF16), "chi", 1)
    y_a = swap((y_a.astype(F32) + far_a.astype(F32)).astype(BF16), "chi", 2)
    x_a, y_b, pieces[1], pieces[2] = after((x_a, y_b, pieces[1], pieces[2]))
    pieces[2], pieces[1] = swap(pieces[2], "dl", 2), swap(pieces[1], "dl", 1)
    env_new = jnp.transpose(run_env(own, x_a, y_a, x_b, y_b, leg_width), (1, 0, 2))
    new_left = jnp.transpose(run_place(pieces, rows, leg_width), (1, 0, 2))
    return (env_new[None], new_left[None])


def from_behind(block, axis, distance):
    devices = range(lax.axis_size(axis))
    route = [((i - distance) % len(devices), i) for i in devices]
    return lax.ppermute(block, axis, route)


def pick(rows, cols, row_of, col_of):
    r = lax.broadcasted_iota(jnp.int32, (rows, cols), 0)
    c = lax.broadcasted_iota(jnp.int32, (rows, cols), 1)
    return (row_of(r) == col_of(c)).astype(BF16)


def double_layer(tensor, pad):
    leg = tensor.shape[0]
    two = leg * leg
    phys = tensor.shape[4]
    big = two * pad

    def outer(first):
        def code(n):
            m, s = n // pad, n % pad
            a = m // leg if first else m % leg
            b = s // leg if first else s % leg
            return jnp.where(s < two, a * leg + b, -1)

        return code

    def same(n):
        return n

    total = None
    ket_rows = pick(big, two, outer(True), same)
    bra_rows = pick(big, two, outer(False), same)
    for p in range(phys):
        mat = tensor[:, :, :, :, p].reshape(two, two)
        ket_small = jnp.dot(ket_rows, mat, preferred_element_type=F32).astype(BF16)
        bra_small = jnp.dot(bra_rows, mat, preferred_element_type=F32).astype(BF16)
        ket = lax.dot_general(ket_small, ket_rows, (((1,), (1,)), ((), ())), preferred_element_type=F32)
        bra = lax.dot_general(bra_small, bra_rows, (((1,), (1,)), ((), ())), preferred_element_type=F32)
        total = ket * bra if total is None else total + ket * bra
    return total.astype(BF16)


def through_site(env, stacked, layer, pad):
    two = env.shape[2]
    summed = jnp.einsum("abm,asc->bmsc", env, stacked, preferred_element_type=F32).astype(BF16)
    amount, columns = summed.shape[0], summed.shape[3]
    flat = summed.reshape(amount, two * pad, columns)
    out = jnp.einsum("tn,btc->bnc", layer, flat, preferred_element_type=F32).astype(BF16)
    return out.reshape(amount, two, pad, columns)


def shards(left_env, up_left, up_center, right_env, center, ket_tensor):
    env_local = left_env[0]
    left_iso = up_left[0]
    left_mid = up_center[0]
    env_right = right_env[0]
    bond_mat = center[0]
    site_ket = ket_tensor[0]
    chi_all = env_local.shape[0]
    leg_width = env_local.shape[2]
    pad = -(-leg_width // 8) * 8
    widen = ((0, 0), (0, pad - leg_width), (0, 0))
    rows = left_iso.shape[0]
    col_count = left_iso.shape[2]

    mid_all = lax.all_gather(left_mid, "chi", axis=0, tiled=True)
    iso_all = lax.all_gather(left_iso, "chi", axis=0, tiled=True)
    next_iso = from_behind(left_iso, "cell", -1)
    bra_iso = lax.all_gather(next_iso, "dl", axis=2, tiled=True)

    layer = double_layer(site_ket, pad)

    mixed = jnp.einsum("abm,ax->bmx", env_local, bond_mat, preferred_element_type=F32).astype(BF16)
    bond_term = jnp.einsum("bma,amc->bc", mixed, env_right, preferred_element_type=F32)
    bond_slots = lax.dynamic_update_slice(
        jnp.zeros((chi_all, chi_all), F32), bond_term, (lax.axis_index("chi") * rows, 0)
    )
    bond_full = lax.psum(bond_slots, ("chi", "dl")).astype(BF16)

    right_cut = through_site(env_local, jnp.pad(mid_all, widen), layer, pad)
    center_term = jnp.einsum(
        "bmda,amc->bdc", right_cut[:, :, :leg_width], env_right, preferred_element_type=F32
    ).astype(BF16)
    iso_all, center_term = lax.optimization_barrier((iso_all, center_term))
    center_part = lax.psum_scatter(center_term, "dl", scatter_dimension=0, tiled=True)
    cross = lax.psum(
        jnp.einsum("bdc,bdy->cy", center_part, center_part, preferred_element_type=F32),
        ("chi", "dl"),
    )
    center_all = lax.all_gather(center_part, "dl", axis=0, tiled=True)

    left_cut = through_site(env_local, jnp.pad(iso_all, widen), layer, pad)
    env_term = jnp.einsum(
        "bmdc,bdk->kmc", left_cut[:, :, :leg_width], bra_iso, preferred_element_type=F32
    ).astype(BF16)
    env_new = lax.psum_scatter(env_term, "chi", scatter_dimension=0, tiled=True).astype(F32)

    bond_wide = bond_full.astype(F32)
    gram = jnp.dot(
        jnp.dot(bond_wide, cross, precision=HIGH), bond_wide.T, precision=HIGH
    )
    one = jnp.eye(chi_all, dtype=F32)
    norm_sum = jnp.sum(gram * one)
    factor = 0.25 * math.sqrt(chi_all) / jnp.sqrt(norm_sum)
    gram = gram * (factor * factor)
    product = None
    for sweep_index in range(ITERS):
        step = 1.5 * one - 0.5 * gram
        product = step if product is None else jnp.dot(product, step, precision=HIGH)
        if sweep_index < ITERS - 1:
            gram = jnp.dot(jnp.dot(step, gram, precision=HIGH), step, precision=HIGH)
    mine = lax.dynamic_slice_in_dim(product, lax.axis_index("dl") * col_count, col_count, 1)
    weight = lax.dot_general(bond_wide, mine, (((0,), (0,)), ((), ())), precision=HIGH)
    weight = weight * (factor * math.sqrt(chi_all * leg_width))
    new_left = jnp.einsum("bdc,cx->bdx", center_all.astype(F32), weight, precision=HIGH)
    return (env_new[None], new_left[None])


def solution(mesh):
    placed = (
        P("cell", None, "chi", None),
        P("cell", "chi", None, "dl"),
        P("cell", "chi", None, "dl"),
        P("cell", "dl", None, None),
        P("cell", None, "dl"),
        P("cell", None, None, None, None, None),
    )
    fits = mesh.shape["chi"] == 4 and mesh.shape["dl"] == 4 and mesh.shape["cell"] == 2
    return jax.shard_map(
        fast if fits else shards,
        mesh=mesh,
        in_specs=placed,
        out_specs=(P("cell", "chi", None, "dl"), P("cell", "chi", None, "dl")),
        check_vma=False,
    )
```

```python
import functools
import math

import jax
import jax.numpy as jnp
from jax import lax
from jax.experimental import pallas as pl
from jax.experimental.pallas import tpu as pltpu
from jax.sharding import PartitionSpec as P

ITERS = 5
HIGH = lax.Precision.HIGH
F32 = jnp.float32
BF16 = jnp.bfloat16
PADM = 40
MIB = 1024 * 1024


def swap(block, axis, distance):
    n = lax.axis_size(axis)
    return lax.ppermute(block, axis, [(i, i ^ distance) for i in range(n)])


def other_cell(block):
    n = lax.axis_size("cell")
    return lax.ppermute(block, "cell", [(i, (i + n - 1) % n) for i in range(n)])


GROUP = 8
LANES = GROUP * 128


def store_x(t, lhs, rhs, xw, count):
    x = jnp.dot(lhs, rhs, preferred_element_type=F32)
    for b in range(count):
        rows = x[b * PADM : (b + 1) * PADM]
        g = b % GROUP
        xw[b // GROUP, t, :, g * 128 : (g + 1) * 128] = jnp.concatenate(
            [rows[:, :128], rows[:, 128:]], axis=0
        ).astype(BF16)


def apply_site(w1_ref, w2_ref, xw, hs, y_ref, count):
    def group(p, carry):
        rows = pl.ds(pl.multiple_of(p * PADM * GROUP, PADM * GROUP), PADM * GROUP)
        for vp in range(3):
            both = []
            for v in (2 * vp, 2 * vp + 1):
                x = xw[p, 3 * v : 3 * v + 3].reshape(6 * PADM, LANES)
                both.append(jnp.dot(w1_ref[...], x, preferred_element_type=F32))
            for k in range(6):
                hs[k, vp * 144 : (vp + 1) * 144, :] = jnp.concatenate(
                    [h[k * 72 : (k + 1) * 72] for h in both], axis=0
                ).astype(BF16)
        for k in range(6):
            y = jnp.dot(w2_ref[...], hs[k], preferred_element_type=F32)
            for l in range(6):
                part = y[l * PADM : (l + 1) * PADM]
                m = k * 6 + l
                y_ref[rows, m * 128 : (m + 1) * 128] = jnp.concatenate(
                    [part[:, g * 128 : (g + 1) * 128] for g in range(GROUP)], axis=0
                ).astype(BF16)
        return carry

    lax.fori_loop(0, count // GROUP, group, 0)


def center_kernel(
    count, env_ref, u0, a1, b1, a2, b2, a3, b3, w1_ref, w2_ref, right_ref, o0, o1, o2, o3, xw, hs, yc, re_ref, sem
):
    me = lax.axis_index("chi")
    z = lax.axis_index("dl")
    fetch = pltpu.make_async_copy(right_ref, re_ref, sem)

    @pl.when(pl.program_id(0) == 0)
    def _():
        fetch.start()

    width = u0.shape[1]
    cut = a1.shape[0]

    def column(leg):
        if leg < cut:
            others = [ref[leg] for ref in (a1, a2, a3)]
        else:
            others = [ref[leg - cut] for ref in (b1, b2, b3)]
        return jnp.concatenate([u0[leg], *others], axis=0)

    for t in range(u0.shape[0] // 2):
        lhs = jnp.concatenate(
            [
                env_ref[:, pl.ds(pl.multiple_of((me ^ d) * width, width), width)]
                for d in range(4)
            ],
            axis=1,
        )
        leg = t % 3 * 12 + t // 3
        rhs = jnp.concatenate([column(leg), column(leg + 6)], axis=1)
        store_x(t, lhs, rhs, xw, count)
    apply_site(w1_ref, w2_ref, xw, hs, yc, count)

    @pl.when(pl.program_id(0) == 0)
    def _():
        fetch.wait()

    result = jnp.dot(yc[...], re_ref[...], preferred_element_type=F32).astype(BF16)
    owner = pl.program_id(0) ^ z
    for d, out in enumerate((o0, o1, o2, o3)):

        @pl.when(owner == d)
        def _(out=out):
            out[...] = result


def left_kernel(
    count, first, last, env_ref, up_ref, w1_ref, w2_ref, bra_ref, *rest
):
    rest = list(rest)
    before = None if first else rest.pop(0)
    outs = [rest.pop(0) for _ in range(7 if last else 1)]
    xw, hs, yl, acc, sem_in, sem_out = rest
    me = lax.axis_index("chi")
    step = pl.program_id(0)
    steps = pl.num_programs(0)

    if not first:

        @pl.when(step == 0)
        def _():
            pltpu.make_async_copy(before, acc, sem_in).start()

    unroll = 6

    def form(s, carry):
        for i in range(unroll):
            leg = i % 3 * 12 + s * (unroll // 3) + i // 3
            rhs = jnp.concatenate(
                [
                    jnp.concatenate([up_ref[d, leg + n] for d in range(up_ref.shape[0])], axis=0)
                    for n in (0, 6)
                ],
                axis=1,
            )
            store_x(s * unroll + i, env_ref[...], rhs, xw, count)
        return carry

    lax.fori_loop(0, up_ref.shape[1] // (2 * unroll), form, 0)
    apply_site(w1_ref, w2_ref, xw, hs, yl, count)

    if not first:

        @pl.when(step == 0)
        def _():
            pltpu.make_async_copy(before, acc, sem_in).wait()

    size = 768
    chunks = yl.shape[1] // size

    def save(n):
        cols = pl.ds(pl.multiple_of(n * size, size), size)
        return pltpu.make_async_copy(acc.at[:, cols], outs[0].at[:, cols], sem_out.at[n])

    def chunk(n, carry):
        cols = pl.ds(pl.multiple_of(n * size, size), size)
        part = jnp.dot(bra_ref[...], yl[:, cols], preferred_element_type=F32)
        if first:

            @pl.when(step == 0)
            def _():
                acc[:, cols] = part

            @pl.when(step > 0)
            def _():
                acc[:, cols] += part
        else:
            acc[:, cols] += part
        if not last:

            @pl.when(step == steps - 1)
            def _():
                save(n).start()

        return carry

    lax.fori_loop(0, chunks, chunk, 0)

    @pl.when(step == steps - 1)
    def _():
        if last:
            width = acc.shape[0] // 8
            outs[0][...] = acc[pl.ds(pl.multiple_of(me * 2 * width, 2 * width), 2 * width), :]
            for n, out in enumerate(outs[1:]):
                place = ((me ^ (n // 2 + 1)) * 2 + n % 2) * width
                rows = pl.ds(pl.multiple_of(place, width), width)
                out[...] = acc[rows, :].astype(out.dtype)
        else:
            for n in range(chunks):
                save(n).wait()


def whole_spec(shape):
    zeros = (0,) * len(shape)
    return pl.BlockSpec(shape, lambda i: zeros, pipeline_mode=pl.Buffered(1))


def cost(amount):
    return pl.CostEstimate(
        flops=int(amount * 0.8e9), bytes_accessed=20 * MIB, transcendentals=0
    )


def run_center(env_rows, ups, w1, w2, re_flat, start, amount):
    count = amount // 4
    block = count * PADM
    wide = re_flat.shape[1]
    return pl.pallas_call(
        functools.partial(center_kernel, count),
        grid=(amount // count,),
        out_shape=[jax.ShapeDtypeStruct((block, wide), BF16)] * 4,
        in_specs=[pl.BlockSpec((block, env_rows.shape[1]), lambda i: (i + start // count, 0))]
        + [whole_spec(u.shape) for u in ups]
        + [whole_spec(w1.shape), whole_spec(w2.shape), pl.BlockSpec(memory_space=pl.ANY)],
        out_specs=[whole_spec((block, wide))] * 4,
        scratch_shapes=[
            pltpu.VMEM((count // GROUP, 18, 2 * PADM, LANES), BF16),
            pltpu.VMEM((6, 432, LANES), BF16),
            pltpu.VMEM((block, 36 * 128), BF16),
            pltpu.VMEM(re_flat.shape, BF16),
            pltpu.SemaphoreType.DMA,
        ],
        compiler_params=pltpu.CompilerParams(vmem_limit_bytes=58 * MIB),
        cost_estimate=cost(amount),
        name="center_path",
    )(env_rows, *ups, w1, w2, re_flat)


def run_left(env_rows, ups, w1, w2, bra, before, start, amount, last):
    count = 32
    block = count * PADM
    chi_all = env_rows.shape[1]
    wide = 36 * 128
    first = before is None
    in_specs = (
        [pl.BlockSpec((block, chi_all), lambda i: (i + start // count, 0))]
        + [whole_spec(ups.shape), whole_spec(w1.shape), whole_spec(w2.shape)]
        + [pl.BlockSpec((bra.shape[0], block), lambda i: (0, i + start // count))]
    )
    args = [env_rows, ups, w1, w2, bra]
    if not first:
        in_specs.append(pl.BlockSpec(memory_space=pl.ANY))
        args.append(before)
    if last:
        own, piece = (chi_all // 4, wide), (chi_all // 8, wide)
        out_shape = [jax.ShapeDtypeStruct(own, F32)] + [jax.ShapeDtypeStruct(piece, BF16)] * 6
        out_specs = [whole_spec(own)] + [whole_spec(piece)] * 6
    else:
        out_shape = jax.ShapeDtypeStruct((chi_all, wide), F32)
        out_specs = pl.BlockSpec(memory_space=pl.ANY)
    return pl.pallas_call(
        functools.partial(left_kernel, count, first, last),
        grid=(amount // count,),
        out_shape=out_shape,
        in_specs=in_specs,
        out_specs=out_specs,
        scratch_shapes=[
            pltpu.VMEM((count // GROUP, 18, 2 * PADM, LANES), BF16),
            pltpu.VMEM((6, 432, LANES), BF16),
            pltpu.VMEM((block, wide), BF16),
            pltpu.VMEM((chi_all, wide), F32),
            pltpu.SemaphoreType.DMA,
            pltpu.SemaphoreType.DMA((wide // 768,)),
        ],
        compiler_params=pltpu.CompilerParams(vmem_limit_bytes=60 * MIB),
        cost_estimate=cost(amount),
        name="left_path",
    )(*args)


def split(x):
    high = x.astype(BF16)
    return high, (x - high.astype(F32)).astype(BF16)


def product_of(a, b):
    (ah, al), (bh, bl) = split(a), split(b)
    small = jnp.dot(ah, bl, preferred_element_type=F32) + jnp.dot(
        al, bh, preferred_element_type=F32
    )
    return small + jnp.dot(ah, bh, preferred_element_type=F32)


def polar_kernel(scale, bond_ref, cross_ref, center_ref, p0, p1, p2, p3, hold):
    n = bond_ref.shape[0]
    cols = p0.shape[1]
    z = lax.axis_index("dl")
    bond = bond_ref[...]
    turned = (((1,), (1,)), ((), ()))
    high, low = split(cross_ref[...])
    half = jnp.dot(bond, high, preferred_element_type=F32) + jnp.dot(
        bond, low, preferred_element_type=F32
    )
    high, low = split(half)
    half = lax.dot_general(high, bond, turned, preferred_element_type=F32) + lax.dot_general(
        low, bond, turned, preferred_element_type=F32
    )
    gram = half + half.T
    same = lax.broadcasted_iota(jnp.int32, (n, n), 0) == lax.broadcasted_iota(
        jnp.int32, (n, n), 1
    )
    trace = jnp.sum(jnp.where(same, gram, 0.0), axis=1, keepdims=True)
    trace = jnp.sum(trace, axis=0, keepdims=True)
    factor = 0.25 * math.sqrt(n) / jnp.sqrt(trace)
    gram = gram * (factor * factor)
    diagonal = jnp.where(same, 1.5, 0.0)
    result = None
    for sweep_index in range(ITERS):
        step = diagonal - 0.5 * gram
        result = step if result is None else product_of(result, step)
        if sweep_index < ITERS - 1:
            gram = product_of(product_of(step, gram), step)
    hold[...] = result
    high, low = split(
        jnp.concatenate(
            [hold[:, pl.ds(pl.multiple_of((z ^ d) * cols, cols), cols)] for d in range(4)],
            axis=1,
        )
    )
    inner = (((0,), (0,)), ((), ()))
    weight = lax.dot_general(bond, high, inner, preferred_element_type=F32)
    weight = weight + lax.dot_general(bond, low, inner, preferred_element_type=F32)
    weight = (weight * (factor * scale)).astype(BF16)
    y = jnp.dot(center_ref[...], weight, preferred_element_type=F32).astype(BF16)
    for d, out in enumerate((p0, p1, p2, p3)):
        out[...] = y[:, d * cols : (d + 1) * cols]


def run_polar(bond, cross, center, scale, cols):
    n = bond.shape[0]
    return pl.pallas_call(
        functools.partial(polar_kernel, scale),
        out_shape=[jax.ShapeDtypeStruct((center.shape[0], cols), BF16)] * 4,
        scratch_shapes=[pltpu.VMEM((n, n), F32)],
        compiler_params=pltpu.CompilerParams(vmem_limit_bytes=58 * MIB),
        cost_estimate=pl.CostEstimate(flops=1000, bytes_accessed=1000, transcendentals=0),
        name="polar",
    )(bond, cross, center)


def place_kernel(p0, p1, p2, p3, out_ref):
    z = lax.axis_index("dl")
    legs, rows, _ = out_ref.shape
    own = rows // 8
    for d, ref in enumerate((p0, p1, p2, p3)):
        for n in range(0, 2 * own, 2):
            pair = ref[n * PADM : (n + 2) * PADM, :].astype(F32)
            row = n // own * (rows // 2) + (z ^ d) * own + n % own
            out_ref[:, row, :] = pair[:legs]
            out_ref[:, row + 1, :] = pair[PADM : PADM + legs]


def run_place(parts, rows, legs):
    return pl.pallas_call(
        place_kernel,
        out_shape=jax.ShapeDtypeStruct((legs, rows, parts[0].shape[1]), F32),
        compiler_params=pltpu.CompilerParams(vmem_limit_bytes=58 * MIB),
        name="new_rows",
    )(*parts)


def env_kernel(own_ref, a1, a2, b1, b2, out_ref):
    cols = out_ref.shape[2]

    def add(one, two):
        for m in range(out_ref.shape[0]):
            lanes = slice(m * cols, (m + 1) * cols)
            part = one[:, lanes].astype(F32) + two[:, lanes].astype(F32)
            out_ref[m] = own_ref[:, lanes] + part

    @pl.when(pl.program_id(0) < 2)
    def _():
        add(a1, a2)

    @pl.when(pl.program_id(0) >= 2)
    def _():
        add(b1, b2)


def run_env(own, a1, a2, b1, b2, legs):
    rows, wide = own.shape
    size = rows // 4
    low = pl.BlockSpec((size, wide), lambda i: (jnp.minimum(i, 1), 0))
    high = pl.BlockSpec((size, wide), lambda i: (jnp.maximum(i - 2, 0), 0))
    return pl.pallas_call(
        env_kernel,
        grid=(4,),
        out_shape=jax.ShapeDtypeStruct((legs, rows, wide // legs), F32),
        in_specs=[pl.BlockSpec((size, wide), lambda i: (i, 0)), low, low, high, high],
        out_specs=pl.BlockSpec((legs, size, wide // legs), lambda i: (0, i, 0)),
        compiler_params=pltpu.CompilerParams(vmem_limit_bytes=58 * MIB),
        name="new_env",
    )(own, a1, a2, b1, b2)


def one_hot(rows, cols, row_of, col_of):
    r = lax.broadcasted_iota(jnp.int32, (rows, cols), 0)
    c = lax.broadcasted_iota(jnp.int32, (rows, cols), 1)
    return row_of(r) == col_of(c)


def site_matrices(ket):
    g, phys = ket.shape[0], ket.shape[4]
    two, wp = g * g, g * phys
    tall, wide = two * wp, g * PADM

    def spread(mat, left, right, keep):
        rows = jnp.dot(left.astype(BF16), mat, preferred_element_type=F32).astype(BF16)
        full = jnp.dot(rows, right.astype(BF16), preferred_element_type=F32)
        return jnp.where(keep, full, 0.0).astype(BF16)

    def same(n):
        return n

    one = jnp.transpose(ket, (2, 3, 4, 1, 0)).reshape(two * phys, two)
    w1 = spread(
        one,
        one_hot(tall, two * phys, lambda n: n // (g * wp) * wp + n % wp, same),
        one_hot(two, wide, same, lambda q: jnp.where(q % PADM < two, q // PADM * g + q % PADM // g, -1)),
        one_hot(tall, wide, lambda n: n // wp % g, lambda q: q % PADM % g),
    )
    other = jnp.transpose(ket, (2, 3, 1, 0, 4)).reshape(two, two * phys)
    w2 = spread(
        other,
        one_hot(wide, two, lambda n: jnp.where(n % PADM < two, n // PADM * g + n % PADM % g, -1), same),
        one_hot(two * phys, tall, same, lambda q: q // wp * phys + q % phys),
        one_hot(wide, tall, lambda n: n % PADM // g, lambda q: q % wp // phys),
    )
    return w1, w2


def fast(left_env, up_left, up_center, right_env, center, ket_tensor):
    env_local = left_env[0]
    left_iso = up_left[0]
    left_mid = up_center[0]
    env_right = right_env[0]
    bond_mat = center[0]
    site_ket = ket_tensor[0]
    chi_all, rows, leg_width = env_local.shape
    cols = left_iso.shape[2]
    z = lax.axis_index("dl")
    me = lax.axis_index("chi")
    after = lax.optimization_barrier

    def add_up(parts):
        total = parts[0].astype(F32)
        for part in parts[1:]:
            total = total + part.astype(F32)
        return total

    bra = jnp.pad(left_iso, ((0, 0), (0, PADM - leg_width), (0, 0)))
    bra = other_cell(bra.reshape(rows * PADM, cols).T)
    mid = jnp.transpose(left_mid, (1, 0, 2))
    env_local, env_right, left_iso, site_ket, bra, mid = after((env_local, env_right, left_iso, site_ket, bra, mid))
    bra_all = lax.all_gather(bra, "dl", axis=0, tiled=True)
    cut = leg_width // 2
    low, high = mid[:cut], mid[cut:]
    low2, high1 = swap(low, "chi", 2), swap(high, "chi", 1)
    low1, high2 = swap(low, "chi", 1), swap(high, "chi", 2)
    w1, w2 = site_matrices(site_ket)
    env_rows = jnp.pad(
        jnp.transpose(env_local, (1, 2, 0)), ((0, 0), (0, PADM - leg_width), (0, 0))
    ).reshape(rows * PADM, chi_all)
    env_rows, low2, high1 = after((env_rows, low2, high1))
    low3, high3 = swap(low2, "chi", 1), swap(high1, "chi", 2)
    mids = [mid, low1, high1, low2, high2, low3, high3]
    re_flat = jnp.transpose(env_right, (1, 0, 2)).reshape(leg_width * cols, chi_all)
    mixed = jnp.dot(env_rows, bond_mat, preferred_element_type=F32).astype(BF16)
    mixed = mixed.reshape(rows, PADM, cols)[:, :leg_width].reshape(rows, leg_width * cols)
    bond = jnp.dot(mixed, re_flat, preferred_element_type=F32)
    iso = jnp.transpose(left_iso, (1, 0, 2))

    w1, w2, iso, bond, env_rows, *mids = after((w1, w2, iso, bond, env_rows, *mids))
    bond_in = swap(bond, "dl", 1)
    half = rows // 2
    terms_a = run_center(env_rows, mids, w1, w2, re_flat, 0, half)

    bond, bond_in, bra_all, iso, *terms_a = after((bond, bond_in, bra_all, iso, *terms_a))
    isos = lax.all_gather(iso, "chi", axis=0)
    bond = bond + bond_in
    got_a = [terms_a[0]] + [swap(terms_a[d], "dl", d) for d in (1, 2, 3)]
    bond_in = swap(bond, "dl", 2)
    env_rows, bond, *mids = after((env_rows, bond, *mids))
    terms_b = run_center(env_rows, mids, w1, w2, re_flat, half, half)

    bond, bond_in, env_rows, *both = after((bond, bond_in, env_rows, *terms_b, *got_a))
    terms_b, got_a = both[:4], both[4:]
    bond = (bond + bond_in).astype(BF16)
    got_b = [terms_b[0]] + [swap(terms_b[d], "dl", d) for d in (1, 2, 3)]
    bond_in = swap(bond, "chi", 1)
    own_a = add_up(got_a).astype(BF16)
    env_rows, bond, own_a = after((env_rows, bond, own_a))
    acc = run_left(env_rows, isos, w1, w2, bra_all, None, 0, half, False)

    acc, bond, bond_in, *got_b = after((acc, bond, bond_in, *got_b))
    own_b = add_up(got_b).astype(BF16)
    own_center = jnp.concatenate([own_a, own_b], axis=0)
    cross = lax.dot_general(
        own_center, own_center, (((0,), (0,)), ((), ())), preferred_element_type=F32
    )
    def exchange(block, axis):
        block = block.astype(BF16)
        return [block] + [swap(block, axis, d) for d in (1, 2, 3)]

    def total_of(c0, c1, c2, c3):
        return (c0.astype(F32) + c1.astype(F32)) + (c2.astype(F32) + c3.astype(F32))

    upper = [cross[n * rows : (n + 1) * rows, n * rows :] for n in range(4)]
    cross = jnp.concatenate(upper, axis=1)
    crosses = exchange(cross, "chi")
    bond = jnp.concatenate([bond, bond_in], axis=0)
    bond_in = swap(bond, "chi", 2)
    acc, cross, bond = after((acc, cross, bond))
    quarter = half // 2
    acc = run_left(env_rows, isos, w1, w2, bra_all, acc, half, quarter, False)

    acc, bond, bond_in, *crosses = after((acc, bond, bond_in, *crosses))
    cross = total_of(*crosses)
    crosses = exchange(cross, "dl")
    acc, cross = after((acc, cross))
    sums = run_left(env_rows, isos, w1, w2, bra_all, acc, half + quarter, quarter, True)

    sums, crosses = list(sums), list(crosses)
    *sums, c0, c1, c2, c3 = after((*sums, *crosses))
    cross = total_of(c0, c1, c2, c3)
    own, x_a, x_b, y_a, y_b, far_a, far_b = sums
    far_a, far_b = swap(far_a, "chi", 1), swap(far_b, "chi", 2)
    x_a, y_b = swap(x_a, "chi", 1), swap(y_b, "chi", 2)

    def by_index(blocks):
        both = jnp.stack(blocks)
        return [lax.dynamic_index_in_dim(both, me ^ d, 0, False) for d in range(4)]

    blocks, start = [], 0
    for n in range(4):
        stop = start + (4 - n) * rows
        blocks.append(
            jnp.concatenate(
                [
                    jnp.zeros((rows, n * rows), F32),
                    0.5 * cross[:, start : start + rows],
                    cross[:, start + rows : stop],
                ],
                axis=1,
            )
        )
        start = stop
    cross = jnp.concatenate(blocks, axis=0)
    bond = jnp.concatenate([bond, bond_in], axis=0).reshape(4, rows, chi_all)
    bond_full = jnp.concatenate(by_index(list(bond)), axis=0)

    pieces = run_polar(
        bond_full, cross, own_center, math.sqrt(chi_all * leg_width), cols
    )
    far_a, far_b, *pieces = after((far_a, far_b, *pieces))
    pieces[3] = swap(pieces[3], "dl", 3)
    x_b = swap((x_b.astype(F32) + far_b.astype(F32)).astype(BF16), "chi", 1)
    y_a = swap((y_a.astype(F32) + far_a.astype(F32)).astype(BF16), "chi", 2)
    x_a, y_b, pieces[1], pieces[2] = after((x_a, y_b, pieces[1], pieces[2]))
    pieces[2], pieces[1] = swap(pieces[2], "dl", 2), swap(pieces[1], "dl", 1)
    env_new = jnp.transpose(run_env(own, x_a, y_a, x_b, y_b, leg_width), (1, 0, 2))
    env_new, *pieces = after((env_new, *pieces))
    new_left = jnp.transpose(run_place(pieces, rows, leg_width), (1, 0, 2))
    return (env_new[None], new_left[None])


def from_behind(block, axis, distance):
    devices = range(lax.axis_size(axis))
    route = [((i - distance) % len(devices), i) for i in devices]
    return lax.ppermute(block, axis, route)


def pick(rows, cols, row_of, col_of):
    r = lax.broadcasted_iota(jnp.int32, (rows, cols), 0)
    c = lax.broadcasted_iota(jnp.int32, (rows, cols), 1)
    return (row_of(r) == col_of(c)).astype(BF16)


def double_layer(tensor, pad):
    leg = tensor.shape[0]
    two = leg * leg
    phys = tensor.shape[4]
    big = two * pad

    def outer(first):
        def code(n):
            m, s = n // pad, n % pad
            a = m // leg if first else m % leg
            b = s // leg if first else s % leg
            return jnp.where(s < two, a * leg + b, -1)

        return code

    def same(n):
        return n

    total = None
    ket_rows = pick(big, two, outer(True), same)
    bra_rows = pick(big, two, outer(False), same)
    for p in range(phys):
        mat = tensor[:, :, :, :, p].reshape(two, two)
        ket_small = jnp.dot(ket_rows, mat, preferred_element_type=F32).astype(BF16)
        bra_small = jnp.dot(bra_rows, mat, preferred_element_type=F32).astype(BF16)
        ket = lax.dot_general(ket_small, ket_rows, (((1,), (1,)), ((), ())), preferred_element_type=F32)
        bra = lax.dot_general(bra_small, bra_rows, (((1,), (1,)), ((), ())), preferred_element_type=F32)
        total = ket * bra if total is None else total + ket * bra
    return total.astype(BF16)


def through_site(env, stacked, layer, pad):
    two = env.shape[2]
    summed = jnp.einsum("abm,asc->bmsc", env, stacked, preferred_element_type=F32).astype(BF16)
    amount, columns = summed.shape[0], summed.shape[3]
    flat = summed.reshape(amount, two * pad, columns)
    out = jnp.einsum("tn,btc->bnc", layer, flat, preferred_element_type=F32).astype(BF16)
    return out.reshape(amount, two, pad, columns)


def shards(left_env, up_left, up_center, right_env, center, ket_tensor):
    env_local = left_env[0]
    left_iso = up_left[0]
    left_mid = up_center[0]
    env_right = right_env[0]
    bond_mat = center[0]
    site_ket = ket_tensor[0]
    chi_all = env_local.shape[0]
    leg_width = env_local.shape[2]
    pad = -(-leg_width // 8) * 8
    widen = ((0, 0), (0, pad - leg_width), (0, 0))
    rows = left_iso.shape[0]
    col_count = left_iso.shape[2]

    mid_all = lax.all_gather(left_mid, "chi", axis=0, tiled=True)
    iso_all = lax.all_gather(left_iso, "chi", axis=0, tiled=True)
    next_iso = from_behind(left_iso, "cell", -1)
    bra_iso = lax.all_gather(next_iso, "dl", axis=2, tiled=True)

    layer = double_layer(site_ket, pad)

    mixed = jnp.einsum("abm,ax->bmx", env_local, bond_mat, preferred_element_type=F32).astype(BF16)
    bond_term = jnp.einsum("bma,amc->bc", mixed, env_right, preferred_element_type=F32)
    bond_slots = lax.dynamic_update_slice(
        jnp.zeros((chi_all, chi_all), F32), bond_term, (lax.axis_index("chi") * rows, 0)
    )
    bond_full = lax.psum(bond_slots, ("chi", "dl")).astype(BF16)

    right_cut = through_site(env_local, jnp.pad(mid_all, widen), layer, pad)
    center_term = jnp.einsum(
        "bmda,amc->bdc", right_cut[:, :, :leg_width], env_right, preferred_element_type=F32
    ).astype(BF16)
    iso_all, center_term = lax.optimization_barrier((iso_all, center_term))
    center_part = lax.psum_scatter(center_term, "dl", scatter_dimension=0, tiled=True)
    cross = lax.psum(
        jnp.einsum("bdc,bdy->cy", center_part, center_part, preferred_element_type=F32),
        ("chi", "dl"),
    )
    center_all = lax.all_gather(center_part, "dl", axis=0, tiled=True)

    left_cut = through_site(env_local, jnp.pad(iso_all, widen), layer, pad)
    env_term = jnp.einsum(
        "bmdc,bdk->kmc", left_cut[:, :, :leg_width], bra_iso, preferred_element_type=F32
    ).astype(BF16)
    env_new = lax.psum_scatter(env_term, "chi", scatter_dimension=0, tiled=True).astype(F32)

    bond_wide = bond_full.astype(F32)
    gram = jnp.dot(
        jnp.dot(bond_wide, cross, precision=HIGH), bond_wide.T, precision=HIGH
    )
    one = jnp.eye(chi_all, dtype=F32)
    norm_sum = jnp.sum(gram * one)
    factor = 0.25 * math.sqrt(chi_all) / jnp.sqrt(norm_sum)
    gram = gram * (factor * factor)
    product = None
    for sweep_index in range(ITERS):
        step = 1.5 * one - 0.5 * gram
        product = step if product is None else jnp.dot(product, step, precision=HIGH)
        if sweep_index < ITERS - 1:
            gram = jnp.dot(jnp.dot(step, gram, precision=HIGH), step, precision=HIGH)
    mine = lax.dynamic_slice_in_dim(product, lax.axis_index("dl") * col_count, col_count, 1)
    weight = lax.dot_general(bond_wide, mine, (((0,), (0,)), ((), ())), precision=HIGH)
    weight = weight * (factor * math.sqrt(chi_all * leg_width))
    new_left = jnp.einsum("bdc,cx->bdx", center_all.astype(F32), weight, precision=HIGH)
    return (env_new[None], new_left[None])


def solution(mesh):
    placed = (
        P("cell", None, "chi", None),
        P("cell", "chi", None, "dl"),
        P("cell", "chi", None, "dl"),
        P("cell", "dl", None, None),
        P("cell", None, "dl"),
        P("cell", None, None, None, None, None),
    )
    fits = mesh.shape["chi"] == 4 and mesh.shape["dl"] == 4 and mesh.shape["cell"] == 2
    return jax.shard_map(
        fast if fits else shards,
        mesh=mesh,
        in_specs=placed,
        out_specs=(P("cell", "chi", None, "dl"), P("cell", "chi", None, "dl")),
        check_vma=False,
    )
```
